32 devices in a mesh: grp: 4 (over z), pen: 8 (over y, x, core).
Axes of the slice: x: 2, y: 2, z: 4, core: 2. Of those that a mesh axis runs over, the one named last changes fastest.
Arguments:
- cell_offsets: int32 [2, 1048576], P(None, ('grp', 'pen')), may hold values from 0 to 1
- cell_z: int32 [1048576], P(('grp', 'pen')), may hold values from 0 to 255
- frac: float32 [3, 1048576], P(None, ('grp', 'pen')), may hold values from 0 to 1
- charges: float32 [1048576], P(('grp', 'pen')), may hold values from -4 to 4
- tile_counts: int32 [16384], P(('grp', 'pen')), may hold values from 16 to 64, as said below
Outputs:
- forces: float32 [3, 1048576], P(None, ('grp', 'pen'))
- energy: float32 [], replicated
The draws below stay inside these ranges and needn't reach their ends.
Inputs may be any that keep to these rules, and one draw needn't show every extreme that they name: `tile_counts`: live slots of each tile; some tile holds 64.
All inputs are finite; a program needn't handle non-finite values.
Results may differ from the reference program's by a relative error of at most 0.0003.
Values sent between devices are 32-bit elements; how exact they have to be, the bound alone decides.
A program may use at most 256 MiB of HBM per device.

```python
import math
import jax
import jax.numpy as jnp
from jax import lax

KX = 256
KY = 256
KZ = 256
SLOTS = 64
TILES = 16384
ATOMS = 1048576
N_GRP = 4
N_PEN = 8


def draw_tile_counts(key, part):
    counts = jax.random.randint(key, (TILES,), max(1, SLOTS // 4), SLOTS + 1)
    filled = jax.random.randint(jax.random.fold_in(key, 7), (), 0, TILES)
    return counts.at[filled].set(SLOTS).astype(jnp.int32)


def place_ends(drawn, key, low, top_value):
    dims = drawn.shape
    spot = [jax.random.randint(jax.random.fold_in(key, axis), (), 0, dims[axis]) for axis in range(len(dims))]
    drawn = drawn.at[tuple(spot)].set(low)
    longest = dims.index(max(dims))
    spot[longest] = (spot[longest] + 1) % dims[longest]
    return drawn.at[tuple(spot)].set(top_value)


def steps_of(own_key, shape, cuts, least, high):
    gain, own = 1.0, jax.random.fold_in(own_key, 6)
    for axis_at, shards_of in cuts:
        steps = jnp.exp(jax.random.uniform(jax.random.fold_in(own, axis_at), (shards_of,), jnp.float32, least / len(cuts), high / len(cuts)))
        gain = gain * jnp.repeat(steps, shape[axis_at] // shards_of).reshape([-1 if axis == axis_at else 1 for axis in range(len(shape))])
    return gain


def scatter_about(stream_key, shape, width, limit, shards=(), kind=jnp.bfloat16):
    array = jax.random.normal(stream_key, shape, jnp.float32) * width
    if len(shards) > 0:
        array = steps_of(stream_key, shape, shards, -0.22, 0.18) * array
    return jnp.clip(array, min=-limit, max=limit).astype(kind)


def setup_inputs(seed: int = 0) -> dict:
    arg_keys = jax.random.split(jax.random.key(seed), 6)
    return {
        "cell_offsets": place_ends(jax.random.randint(arg_keys[0], (2, ATOMS), 0, 2), jax.random.fold_in(arg_keys[0], 1), 0, 1).astype(jnp.int32),
        "cell_z": place_ends(jax.random.randint(arg_keys[1], (ATOMS,), 0, KZ), jax.random.fold_in(arg_keys[1], 1), 0, KZ - 1).astype(jnp.int32),
        "frac": jnp.clip(1.0 * jax.random.uniform(arg_keys[2], (3, ATOMS), jnp.float32) ** steps_of(arg_keys[2], (3, ATOMS), ((1, 32),), -0.2, 0.2), 0.0, 1.0),
        "charges": scatter_about(arg_keys[3], (ATOMS,), 1.0, 4.0, ((0, 32),), jnp.float32),
        "tile_counts": draw_tile_counts(jax.random.fold_in(arg_keys[5], 71), 0),
    }


ewald_split = 0.6


def spline_rows(fracs):
    values = [jnp.ones_like(fracs)]
    fifth = values
    for order in range(2, 7):
        nxt = []
        for j in range(order):
            term = jnp.zeros_like(fracs)
            if j >= 1:
                term = term + values[j - 1] * (fracs + order - 1 - j)
            if j <= order - 2:
                term = term + values[j] * (1.0 - fracs + j)
            nxt.append(term / (order - 1))
        if order == 5:
            fifth = nxt
        values = nxt
    slopes = []
    for j in range(6):
        term = jnp.zeros_like(fracs)
        if j >= 1:
            term = term + fifth[j - 1]
        if j <= 4:
            term = term - fifth[j]
        slopes.append(term)
    return values, slopes


def tile_weights(offsets, zcell, fracs, charge, counts, size_z):
    slots = charge.shape[-1]
    live = (jnp.arange(slots, dtype=jnp.int32) < counts[..., None]).astype(jnp.float32)
    live_q = charge * live
    theta_x, slope_x = spline_rows(fracs[0])
    theta_y, slope_y = spline_rows(fracs[1])
    theta_z, slope_z = spline_rows(fracs[2])
    footing = jnp.arange(8, dtype=jnp.int32)[:, None]
    cells = jnp.arange(size_z, dtype=jnp.int32)
    weight_x = 0.0
    grade_x = 0.0
    weight_y = 0.0
    grade_y = 0.0
    weight_z = 0.0
    grade_z = 0.0
    for j in range(6):
        hit_x = (footing == offsets[0][..., None, :] + j).astype(jnp.float32)
        hit_y = (footing == offsets[1][..., None, :] + j).astype(jnp.float32)
        hit_z = (cells == (zcell[..., :, None] + j) % size_z).astype(jnp.float32)
        weight_x = weight_x + theta_x[j][..., None, :] * hit_x
        grade_x = grade_x + slope_x[j][..., None, :] * hit_x
        weight_y = weight_y + theta_y[j][..., None, :] * hit_y
        grade_y = grade_y + slope_y[j][..., None, :] * hit_y
        weight_z = weight_z + theta_z[j][..., :, None] * hit_z
        grade_z = grade_z + slope_z[j][..., :, None] * hit_z
    return weight_x, grade_x, weight_y, grade_y, weight_z, grade_z, live_q


def modulus(index, length):
    coeffs = (1.0 / 120.0, 26.0 / 120.0, 66.0 / 120.0, 26.0 / 120.0, 1.0 / 120.0)
    real_part = 0.0
    imag_part = 0.0
    for j in range(5):
        angle = ((index * j) % length).astype(jnp.float32) * (2.0 * math.pi / length)
        real_part = real_part + coeffs[j] * jnp.cos(angle)
        imag_part = imag_part + coeffs[j] * jnp.sin(angle)
    return real_part * real_part + imag_part * imag_part


def influence(index_x, index_y, index_z):
    freq_x = jnp.where(2 * index_x < KX, index_x, index_x - KX).astype(jnp.float32) / KX
    freq_y = jnp.where(2 * index_y < KY, index_y, index_y - KY).astype(jnp.float32) / KY
    freq_z = jnp.where(2 * index_z < KZ, index_z, index_z - KZ).astype(jnp.float32) / KZ
    square = freq_x * freq_x + freq_y * freq_y + freq_z * freq_z
    safe = jnp.where(square > 0, square, 1.0)
    volume = float(KX * KY * KZ)
    value = jnp.exp(-(math.pi ** 2) * safe / (ewald_split ** 2)) / (math.pi * volume * safe)
    value = value / (modulus(index_x, KX) * modulus(index_y, KY) * modulus(index_z, KZ))
    return jnp.where(square > 0, value, 0.0)


def reference(cell_offsets, cell_z, frac, charges, tile_counts):
    tiles_x = KX // N_GRP // 2
    tiles_y = KY // N_PEN // 2
    rows_x = KX // 2
    rows_y = KY // 2
    highest = lax.Precision.HIGHEST

    def arrange(arr):
        lead = arr.shape[:-1]
        count = len(lead)
        shaped = arr.reshape(lead + (N_GRP, N_PEN, tiles_x, tiles_y, SLOTS))
        order = tuple(range(count)) + (count, count + 2, count + 1, count + 3, count + 4)
        return jnp.transpose(shaped, order).reshape(lead + (rows_x, rows_y, SLOTS))

    offsets = jnp.moveaxis(arrange(cell_offsets), 1, 0)
    fracs = jnp.moveaxis(arrange(frac), 1, 0)
    zcell = arrange(cell_z)
    charge = arrange(charges)
    counts = jnp.transpose(tile_counts.reshape(N_GRP, N_PEN, tiles_x, tiles_y), (0, 2, 1, 3)).reshape(rows_x, rows_y)
    row_ids = jnp.arange(rows_x, dtype=jnp.int32)
    eight = jnp.arange(8, dtype=jnp.int32)

    def spread_row(grid, inputs):
        offs, zrow, frow, qrow, crow, row = inputs
        weight_x, grade_x, weight_y, grade_y, weight_z, grade_z, live_q = tile_weights(offs, zrow, frow, qrow, crow, KZ)
        pair = (weight_x[:, :, None, :] * weight_y[:, None, :, :] * live_q[:, None, None, :]).reshape(rows_y, 64, SLOTS)
        spread = jnp.einsum("tfs,tsz->tfz", pair, weight_z, precision=highest).reshape(rows_y, 8, 4, 2, KZ)
        slab = 0.0
        for j in range(4):
            part = jnp.transpose(spread[:, :, j], (1, 0, 2, 3))
            slab = slab + jnp.roll(part, j, axis=1).reshape(8, KY, KZ)
        targets = (2 * row + eight) % KX
        return grid.at[targets].add(slab), None

    start = jnp.zeros((KX, KY, KZ), jnp.float32)
    charge_mesh, _ = lax.scan(spread_row, start, (offsets, zcell, fracs, charge, counts, row_ids))
    spectrum = jnp.fft.fftn(charge_mesh)
    index_x = jnp.arange(KX, dtype=jnp.int32)[:, None, None]
    index_y = jnp.arange(KY, dtype=jnp.int32)[None, :, None]
    index_z = jnp.arange(KZ, dtype=jnp.int32)[None, None, :]
    kernel = influence(index_x, index_y, index_z)
    power = jnp.real(spectrum) ** 2 + jnp.imag(spectrum) ** 2
    energy = 0.5 * jnp.sum(kernel * power)
    potential = jnp.real(jnp.fft.ifftn(kernel * spectrum)) * float(KX * KY * KZ)

    def interp_row(carry, inputs):
        offs, zrow, frow, qrow, crow, row = inputs
        weight_x, grade_x, weight_y, grade_y, weight_z, grade_z, live_q = tile_weights(offs, zrow, frow, qrow, crow, KZ)
        rows = jnp.take(potential, (2 * row + eight) % KX, axis=0)
        parts = []
        for j in range(4):
            parts.append(jnp.roll(rows, -2 * j, axis=1).reshape(8, rows_y, 2, KZ))
        footing = jnp.transpose(jnp.stack(parts, axis=0), (2, 1, 0, 3, 4)).reshape(rows_y, 64, KZ)
        main = jnp.einsum("tfz,tsz->tfs", footing, weight_z, precision=highest).reshape(rows_y, 8, 8, SLOTS)
        tilt = jnp.einsum("tfz,tsz->tfs", footing, grade_z, precision=highest).reshape(rows_y, 8, 8, SLOTS)
        force_x = -live_q * jnp.einsum("txs,tys,txys->ts", grade_x, weight_y, main, precision=highest)
        force_y = -live_q * jnp.einsum("txs,tys,txys->ts", weight_x, grade_y, main, precision=highest)
        force_z = -live_q * jnp.einsum("txs,tys,txys->ts", weight_x, weight_y, tilt, precision=highest)
        return carry, jnp.stack([force_x, force_y, force_z], axis=0)

    _, stacked = lax.scan(interp_row, 0.0, (offsets, zcell, fracs, charge, counts, row_ids))
    forces = stacked.reshape(N_GRP, tiles_x, 3, N_PEN, tiles_y, SLOTS)
    forces = jnp.transpose(forces, (2, 0, 3, 1, 4, 5)).reshape(3, ATOMS)
    return forces, (energy / ATOMS).astype(jnp.float32)
```

```python
import functools
import math

import jax
import jax.numpy as jnp
from jax import lax
from jax.experimental import pallas as pl
from jax.experimental.pallas import tpu as pltpu
from jax.sharding import PartitionSpec as P

KX = 256
KY = 256
KZ = 256
ATOMS = 1048576


ewald_split = 0.6
highest = lax.Precision.HIGH


def shifted(block, axis, distance):
    devices = range(lax.axis_size(axis))
    route = [((i - distance) % len(devices), i) for i in devices]
    return lax.ppermute(block, axis, route)


def spline_rows(fracs):
    values = [jnp.ones_like(fracs)]
    fifth = values
    for order in range(2, 7):
        nxt = []
        for j in range(order):
            term = jnp.zeros_like(fracs)
            if j >= 1:
                term = values[j - 1] * (fracs + order - 1 - j)
            if j <= order - 2:
                term = term + values[j] * (1.0 - fracs + j)
            nxt.append(term / (order - 1))
        if order == 5:
            fifth = nxt
        values = nxt
    slopes = []
    for j in range(6):
        term = jnp.zeros_like(fracs)
        if j >= 1:
            term = fifth[j - 1]
        if j <= 4:
            term = term - fifth[j]
        slopes.append(term)
    return (values, slopes)


def select_rows(distance, values):
    total = jnp.zeros(distance.shape, jnp.float32)
    for j in range(6):
        total = jnp.where(distance == j, values[j], total)
    return total


def select_pair(distance, values, grades):
    total = jnp.zeros(distance.shape, jnp.float32)
    slope = jnp.zeros(distance.shape, jnp.float32)
    for j in range(6):
        hit = distance == j
        total = jnp.where(hit, values[j], total)
        slope = jnp.where(hit, grades[j], slope)
    return (total, slope)


def split(values):
    high = values.astype(jnp.bfloat16)
    low = (values - high.astype(jnp.float32)).astype(jnp.bfloat16)
    return (high, low)


def product(high, low, other, dims):
    other_high, other_low = split(other)
    rows = high.shape[0]
    both = lax.dot_general(
        jnp.concatenate([high, low], axis=0), other_high, dims, preferred_element_type=jnp.float32
    )
    rest = lax.dot_general(high, other_low, dims, preferred_element_type=jnp.float32)
    return both[:rows] + both[rows:] + rest


def row_of(values, i):
    return [value[i : i + 1] for value in values]


def y_offset(offset, slots):
    lane = lax.broadcasted_iota(jnp.int32, offset.shape, 1)
    return offset + 2 * (lane // slots)


def spread_kernel(per_row, slots, off_ref, z_ref, frac_ref, q_ref, grid_ref):
    width = z_ref.shape[1]
    size_z = grid_ref.shape[2]
    grid_ref[...] = jnp.zeros_like(grid_ref)

    def step(outer, carry):
        rows = pl.ds(pl.multiple_of(outer * 8, 8), 8)
        theta_x, _ = spline_rows(frac_ref[0, rows, :])
        theta_y, _ = spline_rows(frac_ref[1, rows, :])
        theta_z, _ = spline_rows(frac_ref[2, rows, :])
        charge = q_ref[rows, :]
        theta_x = [theta * charge for theta in theta_x]
        off_x = off_ref[0, rows, :]
        off_y = y_offset(off_ref[1, rows, :], slots)
        base = z_ref[rows, :]
        eight = lax.broadcasted_iota(jnp.int32, (8, width), 0)
        sixteen = lax.broadcasted_iota(jnp.int32, (16, width), 0)
        cells = lax.broadcasted_iota(jnp.int32, (size_z, width), 0)
        for i in range(8):
            weight_x = select_rows(eight - off_x[i : i + 1], row_of(theta_x, i))
            weight_y = select_rows(sixteen - off_y[i : i + 1], row_of(theta_y, i))
            weight_z = select_rows(
                (cells - base[i : i + 1]) & (size_z - 1), row_of(theta_z, i)
            )
            pair = jnp.concatenate([weight_x[k : k + 1] * weight_y for k in range(8)], axis=0)
            high, low = split(pair)
            out = product(high, low, weight_z, (((1,), (1,)), ((), ())))
            first = 2 * (outer * (8 // per_row) + i // per_row)
            y0 = 8 * (i % per_row)
            for k in range(8):
                grid_ref[first + k, y0 : y0 + 16, :] += out[16 * k : 16 * k + 16]
        return carry

    lax.fori_loop(0, z_ref.shape[0] // 8, step, 0)


def interp_kernel(
    per_row, slots, off_ref, z_ref, frac_ref, q_ref, pot_ref, up_ref, side_ref, out_ref, ext_ref
):
    width = z_ref.shape[1]
    size_z = pot_ref.shape[2]
    block_x, block_y = pot_ref.shape[0], pot_ref.shape[1]
    ext_ref[:block_x, :block_y] = pot_ref[...]
    ext_ref[block_x : block_x + 5, :block_y] = up_ref[...]
    ext_ref[block_x + 5 :, :block_y] = jnp.zeros((3, block_y, size_z), jnp.float32)
    ext_ref[: block_x + 5, block_y:] = side_ref[...]
    ext_ref[block_x + 5 :, block_y:] = jnp.zeros((3, 8, size_z), jnp.float32)

    def step(outer, carry):
        rows = pl.ds(pl.multiple_of(outer * 8, 8), 8)
        theta_x, slope_x = spline_rows(frac_ref[0, rows, :])
        theta_y, slope_y = spline_rows(frac_ref[1, rows, :])
        theta_z, slope_z = spline_rows(frac_ref[2, rows, :])
        off_x = off_ref[0, rows, :]
        off_y = y_offset(off_ref[1, rows, :], slots)
        base = z_ref[rows, :]
        eight = lax.broadcasted_iota(jnp.int32, (8, width), 0)
        sixteen = lax.broadcasted_iota(jnp.int32, (16, width), 0)
        cells = lax.broadcasted_iota(jnp.int32, (size_z, width), 0)
        dims = (((1,), (0,)), ((), ()))
        forces = [[], [], []]
        for i in range(8):
            weight_x, grade_x = select_pair(
                eight - off_x[i : i + 1], row_of(theta_x, i), row_of(slope_x, i)
            )
            weight_y, grade_y = select_pair(
                sixteen - off_y[i : i + 1], row_of(theta_y, i), row_of(slope_y, i)
            )
            weight_z, grade_z = select_pair(
                (cells - base[i : i + 1]) & (size_z - 1), row_of(theta_z, i), row_of(slope_z, i)
            )
            first = 2 * (outer * (8 // per_row) + i // per_row)
            y0 = 8 * (i % per_row)
            footing = jnp.concatenate(
                [ext_ref[first + k, y0 : y0 + 16, :] for k in range(8)], axis=0
            )
            high, low = split(footing)
            main = product(high, low, weight_z, dims)
            tilt = product(high, low, grade_z, dims)
            along_x = 0.0
            along_y = 0.0
            along_z = 0.0
            for k in range(8):
                piece = main[16 * k : 16 * k + 16]
                along_x = along_x + grade_x[k : k + 1] * piece
                along_y = along_y + weight_x[k : k + 1] * piece
                along_z = along_z + weight_x[k : k + 1] * tilt[16 * k : 16 * k + 16]
            forces[0].append(jnp.sum(along_x * weight_y, axis=0, keepdims=True))
            forces[1].append(jnp.sum(along_y * grade_y, axis=0, keepdims=True))
            forces[2].append(jnp.sum(along_z * weight_y, axis=0, keepdims=True))
        minus_q = -q_ref[rows, :]
        for d in range(3):
            out_ref[d, rows, :] = minus_q * jnp.concatenate(forces[d], axis=0)
        return carry

    lax.fori_loop(0, z_ref.shape[0] // 8, step, 0)


def modulus(index, length):
    coeffs = (1.0 / 120.0, 26.0 / 120.0, 66.0 / 120.0, 26.0 / 120.0, 1.0 / 120.0)
    real_part = 0.0
    imag_part = 0.0
    for j in range(5):
        angle = (index * j % length).astype(jnp.float32) * (2.0 * math.pi / length)
        real_part = real_part + coeffs[j] * jnp.cos(angle)
        imag_part = imag_part + coeffs[j] * jnp.sin(angle)
    return real_part * real_part + imag_part * imag_part


def influence(index_x, index_y, index_z):
    freq_x = jnp.where(2 * index_x < KX, index_x, index_x - KX).astype(jnp.float32) / KX
    freq_y = jnp.where(2 * index_y < KY, index_y, index_y - KY).astype(jnp.float32) / KY
    freq_z = jnp.where(2 * index_z < KZ, index_z, index_z - KZ).astype(jnp.float32) / KZ
    square = freq_x * freq_x + freq_y * freq_y + freq_z * freq_z
    safe = jnp.where(square > 0, square, 1.0)
    volume = float(KX * KY * KZ)
    value = jnp.exp(-math.pi**2 * safe / ewald_split**2) / (math.pi * volume * safe)
    value = value / (modulus(index_x, KX) * modulus(index_y, KY) * modulus(index_z, KZ))
    return jnp.where(square > 0, value, 0.0)


def dft_tables(length):
    index = jnp.arange(length, dtype=jnp.int32)
    angle = (index[:, None] * index[None, :] % length).astype(jnp.float32) * (
        2.0 * math.pi / length
    )
    return (jnp.cos(angle), jnp.sin(angle))


def z_slots(groups):
    planes = KZ // (2 * groups) + 1
    owner = jnp.arange(groups, dtype=jnp.int32)[:, None]
    within = jnp.arange(planes, dtype=jnp.int32)[None, :]
    ordinary = owner * (planes - 1) + within
    frequency = jnp.where(within < planes - 1, ordinary, jnp.where(owner == 0, KZ // 2, 0))
    plane_weight = jnp.where(
        within < planes - 1, jnp.where(frequency == 0, 1.0, 2.0), jnp.where(owner == 0, 1.0, 0.0)
    )
    frequency = frequency.reshape(-1)
    plane_weight = plane_weight.reshape(-1).astype(jnp.float32)
    position = jnp.arange(KZ, dtype=jnp.int32)
    angle = (frequency[:, None] * position[None, :] % KZ).astype(jnp.float32) * (2.0 * math.pi / KZ)
    usable = (plane_weight > 0).astype(jnp.float32)[:, None]
    return (planes, frequency, plane_weight, jnp.cos(angle) * usable, jnp.sin(angle) * usable)


def forward_complex(data, cos_table, sin_table, shape, axis):
    direct = jnp.dot(cos_table, data, precision=highest).reshape(shape)
    other = jnp.dot(sin_table, data, precision=highest).reshape(shape)
    real_part = jnp.take(direct, 0, axis=axis) + jnp.take(other, 1, axis=axis)
    imag_part = jnp.take(direct, 1, axis=axis) - jnp.take(other, 0, axis=axis)
    return (real_part, imag_part)


def inverse_complex(data, cos_table, sin_table, shape, axis):
    direct = jnp.dot(cos_table, data, precision=highest).reshape(shape)
    other = jnp.dot(sin_table, data, precision=highest).reshape(shape)
    real_part = jnp.take(direct, 0, axis=axis) - jnp.take(other, 1, axis=axis)
    imag_part = jnp.take(other, 0, axis=axis) + jnp.take(direct, 1, axis=axis)
    return (real_part, imag_part)


def spectrum_pen_first(grid, block_x, block_y):
    cos_x, sin_x = dft_tables(KX)
    cos_y, sin_y = dft_tables(KY)
    planes, frequency, plane_weight, cos_z, sin_z = z_slots(lax.axis_size("pen"))
    slot_total = cos_z.shape[0]
    lines = KY // lax.axis_size("grp")
    real_z = jnp.einsum("xyz,kz->ykx", grid, cos_z, precision=highest)
    imag_z = -jnp.einsum("xyz,kz->ykx", grid, sin_z, precision=highest)
    outgoing = jnp.stack([real_z, imag_z], axis=2).reshape(block_y, slot_total * 2 * block_x)
    columns = lax.all_to_all(outgoing, "pen", split_axis=1, concat_axis=0, tiled=True)
    real_y, imag_y = forward_complex(columns, cos_y, sin_y, (KY, planes, 2, block_x), 2)
    sectioned = jnp.transpose(jnp.stack([real_y, imag_y], axis=-1), (2, 0, 1, 3)).reshape(
        block_x, KY * planes * 2
    )
    rows = lax.all_to_all(sectioned, "grp", split_axis=1, concat_axis=0, tiled=True)
    real_x, imag_x = forward_complex(rows, cos_x, sin_x, (KX, lines, planes, 2), 3)
    first = lax.axis_index("pen") * planes
    index_x = jnp.arange(KX, dtype=jnp.int32)[:, None, None]
    index_y = lax.axis_index("grp") * lines + jnp.arange(lines, dtype=jnp.int32)[None, :, None]
    index_z = lax.dynamic_slice_in_dim(frequency, first, planes)[None, None, :]
    local_weight = lax.dynamic_slice_in_dim(plane_weight, first, planes)[None, None, :]
    kernel = influence(index_x, index_y, index_z)
    spectral = 0.5 * jnp.sum(local_weight * kernel * (real_x * real_x + imag_x * imag_x))
    scaled = jnp.stack([kernel * real_x, kernel * imag_x], axis=-1).reshape(KX, lines * planes * 2)
    real_b, imag_b = inverse_complex(scaled, cos_x, sin_x, (KX, lines, planes, 2), 3)
    returning = jnp.stack([real_b, imag_b], axis=-1).reshape(KX, lines * planes * 2)
    rows_home = lax.all_to_all(returning, "grp", split_axis=0, concat_axis=1, tiled=True)
    rows_home = jnp.transpose(rows_home.reshape(block_x, KY, planes, 2), (1, 2, 3, 0)).reshape(
        KY, planes * 2 * block_x
    )
    real_c, imag_c = inverse_complex(rows_home, cos_y, sin_y, (KY, planes, 2, block_x), 2)
    leaving = jnp.stack([real_c, imag_c], axis=2).reshape(KY, planes * 2 * block_x)
    home = lax.all_to_all(leaving, "pen", split_axis=0, concat_axis=1, tiled=True).reshape(
        block_y, slot_total, 2, block_x
    )
    potential = jnp.einsum(
        "ykx,kz->xyz", home[:, :, 0], plane_weight[:, None] * cos_z, precision=highest
    )
    potential = potential - jnp.einsum(
        "ykx,kz->xyz", home[:, :, 1], plane_weight[:, None] * sin_z, precision=highest
    )
    return (potential, spectral)


def local(cell_offsets, cell_z, frac, charges, tile_counts):
    block_x = KX // lax.axis_size("grp")
    block_y = KY // lax.axis_size("pen")
    tiles = tile_counts.shape[0]
    slots = charges.shape[0] // tiles
    width = 4 * slots
    groups = tiles // 4
    per_row = block_y // 8
    live = jnp.arange(slots, dtype=jnp.int32)[None, :] < tile_counts[:, None]
    live_q = (charges.reshape(tiles, slots) * live.astype(jnp.float32)).reshape(groups, width)
    offsets = cell_offsets.reshape(2, groups, width)
    zcell = cell_z.reshape(groups, width)
    fracs = frac.reshape(3, groups, width)
    vmem = pl.BlockSpec(memory_space=pltpu.VMEM)
    params = pltpu.CompilerParams(vmem_limit_bytes=60 * 1024 * 1024)
    padded = pl.pallas_call(
        functools.partial(spread_kernel, per_row, slots),
        out_shape=jax.ShapeDtypeStruct((block_x + 8, block_y + 8, KZ), jnp.float32),
        in_specs=[vmem] * 4,
        out_specs=vmem,
        compiler_params=params,
        name="spread",
    )(offsets, zcell, fracs, live_q)
    rim_y = shifted(padded[: block_x + 5, block_y : block_y + 5], "pen", 1)
    merged = padded[: block_x + 5, :block_y].at[:, :5].add(rim_y)
    rim_x = shifted(merged[block_x : block_x + 5], "grp", 1)
    grid = merged[:block_x].at[:5].add(rim_x)
    potential, spectral = spectrum_pen_first(grid, block_x, block_y)
    upper = shifted(potential[:5], "grp", -1)
    ext_x = jnp.concatenate([potential[:, :5], upper[:, :5]], axis=0)
    beside = shifted(ext_x, "pen", -1)
    beside = jnp.pad(beside, ((0, 0), (0, 3), (0, 0)))
    forces = pl.pallas_call(
        functools.partial(interp_kernel, per_row, slots),
        out_shape=jax.ShapeDtypeStruct((3, groups, width), jnp.float32),
        in_specs=[vmem] * 7,
        out_specs=vmem,
        scratch_shapes=[pltpu.VMEM((block_x + 8, block_y + 8, KZ), jnp.float32)],
        compiler_params=params,
        name="interp",
    )(offsets, zcell, fracs, live_q, potential, upper, beside)
    total = lax.psum(spectral, ("grp", "pen"))
    return (forces.reshape(3, groups * width), total / ATOMS)


def solution(mesh):
    in_specs = (
        P(None, ("grp", "pen")),
        P(("grp", "pen")),
        P(None, ("grp", "pen")),
        P(("grp", "pen")),
        P(("grp", "pen")),
    )
    out_specs = (P(None, ("grp", "pen")), P())
    return jax.shard_map(local, mesh=mesh, in_specs=in_specs, out_specs=out_specs, check_vma=False)
```

```python
import functools
import math

import jax
import jax.numpy as jnp
import numpy as np
from jax import lax
from jax.experimental import pallas as pl
from jax.experimental.pallas import tpu as pltpu
from jax.sharding import PartitionSpec as P

KX = 256
KY = 256
KZ = 256
ATOMS = 1048576


ewald_split = 0.6
highest = lax.Precision.HIGH


def shifted(block, axis, distance):
    devices = range(lax.axis_size(axis))
    route = [((i - distance) % len(devices), i) for i in devices]
    return lax.ppermute(block, axis, route)


def spline_rows(fracs):
    values = [jnp.ones_like(fracs)]
    fifth = values
    for order in range(2, 7):
        nxt = []
        for j in range(order):
            term = jnp.zeros_like(fracs)
            if j >= 1:
                term = values[j - 1] * (fracs + order - 1 - j)
            if j <= order - 2:
                term = term + values[j] * (1.0 - fracs + j)
            nxt.append(term / (order - 1))
        if order == 5:
            fifth = nxt
        values = nxt
    slopes = []
    for j in range(6):
        term = jnp.zeros_like(fracs)
        if j >= 1:
            term = fifth[j - 1]
        if j <= 4:
            term = term - fifth[j]
        slopes.append(term)
    return (values, slopes)


def select_rows(distance, values):
    total = jnp.zeros(distance.shape, jnp.float32)
    for j in range(6):
        total = jnp.where(distance == j, values[j], total)
    return total


def select_pair(distance, values, grades):
    total = jnp.zeros(distance.shape, jnp.float32)
    slope = jnp.zeros(distance.shape, jnp.float32)
    for j in range(6):
        hit = distance == j
        total = jnp.where(hit, values[j], total)
        slope = jnp.where(hit, grades[j], slope)
    return (total, slope)


def split(values):
    high = values.astype(jnp.bfloat16)
    low = (values - high.astype(jnp.float32)).astype(jnp.bfloat16)
    return (high, low)


def product(high, low, other, dims):
    other_high, other_low = split(other)
    rows = high.shape[0]
    both = lax.dot_general(
        jnp.concatenate([high, low], axis=0), other_high, dims, preferred_element_type=jnp.float32
    )
    rest = lax.dot_general(high, other_low, dims, preferred_element_type=jnp.float32)
    return both[:rows] + both[rows:] + rest


def row_of(values, i):
    return [value[i : i + 1] for value in values]


def y_offset(offset, slots):
    lane = lax.broadcasted_iota(jnp.int32, offset.shape, 1)
    return offset + 2 * (lane // slots)


def spread_kernel(per_row, slots, off_ref, z_ref, frac_ref, q_ref, grid_ref):
    width = z_ref.shape[1]
    size_z = grid_ref.shape[2]
    grid_ref[...] = jnp.zeros_like(grid_ref)

    def step(outer, carry):
        rows = pl.ds(pl.multiple_of(outer * 8, 8), 8)
        theta_x, _ = spline_rows(frac_ref[0, rows, :])
        theta_y, _ = spline_rows(frac_ref[1, rows, :])
        theta_z, _ = spline_rows(frac_ref[2, rows, :])
        charge = q_ref[rows, :]
        theta_x = [theta * charge for theta in theta_x]
        off_x = off_ref[0, rows, :]
        off_y = y_offset(off_ref[1, rows, :], slots)
        base = z_ref[rows, :]
        eight = lax.broadcasted_iota(jnp.int32, (8, width), 0)
        sixteen = lax.broadcasted_iota(jnp.int32, (16, width), 0)
        cells = lax.broadcasted_iota(jnp.int32, (size_z, width), 0)
        for i in range(8):
            weight_x = select_rows(eight - off_x[i : i + 1], row_of(theta_x, i))
            weight_y = select_rows(sixteen - off_y[i : i + 1], row_of(theta_y, i))
            weight_z = select_rows(
                (cells - base[i : i + 1]) & (size_z - 1), row_of(theta_z, i)
            )
            pair = jnp.concatenate([weight_x[k : k + 1] * weight_y for k in range(8)], axis=0)
            high, low = split(pair)
            out = product(high, low, weight_z, (((1,), (1,)), ((), ())))
            first = 2 * (outer * (8 // per_row) + i // per_row)
            y0 = 8 * (i % per_row)
            for k in range(8):
                grid_ref[first + k, y0 : y0 + 16, :] += out[16 * k : 16 * k + 16]
        return carry

    lax.fori_loop(0, z_ref.shape[0] // 8, step, 0)


def interp_kernel(
    per_row, slots, off_ref, z_ref, frac_ref, q_ref, pot_ref, up_ref, side_ref, out_ref, ext_ref
):
    width = z_ref.shape[1]
    size_z = pot_ref.shape[2]
    block_x, block_y = pot_ref.shape[0], pot_ref.shape[1]
    ext_ref[:block_x, :block_y] = pot_ref[...]
    ext_ref[block_x : block_x + 5, :block_y] = up_ref[...]
    ext_ref[block_x + 5 :, :block_y] = jnp.zeros((3, block_y, size_z), jnp.float32)
    ext_ref[: block_x + 5, block_y:] = side_ref[...]
    ext_ref[block_x + 5 :, block_y:] = jnp.zeros((3, 8, size_z), jnp.float32)

    def step(outer, carry):
        rows = pl.ds(pl.multiple_of(outer * 8, 8), 8)
        theta_x, slope_x = spline_rows(frac_ref[0, rows, :])
        theta_y, slope_y = spline_rows(frac_ref[1, rows, :])
        theta_z, slope_z = spline_rows(frac_ref[2, rows, :])
        off_x = off_ref[0, rows, :]
        off_y = y_offset(off_ref[1, rows, :], slots)
        base = z_ref[rows, :]
        eight = lax.broadcasted_iota(jnp.int32, (8, width), 0)
        sixteen = lax.broadcasted_iota(jnp.int32, (16, width), 0)
        cells = lax.broadcasted_iota(jnp.int32, (size_z, width), 0)
        dims = (((1,), (0,)), ((), ()))
        forces = [[], [], []]
        for i in range(8):
            weight_x, grade_x = select_pair(
                eight - off_x[i : i + 1], row_of(theta_x, i), row_of(slope_x, i)
            )
            weight_y, grade_y = select_pair(
                sixteen - off_y[i : i + 1], row_of(theta_y, i), row_of(slope_y, i)
            )
            weight_z, grade_z = select_pair(
                (cells - base[i : i + 1]) & (size_z - 1), row_of(theta_z, i), row_of(slope_z, i)
            )
            first = 2 * (outer * (8 // per_row) + i // per_row)
            y0 = 8 * (i % per_row)
            footing = jnp.concatenate(
                [ext_ref[first + k, y0 : y0 + 16, :] for k in range(8)], axis=0
            )
            high, low = split(footing)
            main = product(high, low, weight_z, dims)
            tilt = product(high, low, grade_z, dims)
            along_x = 0.0
            along_y = 0.0
            along_z = 0.0
            for k in range(8):
                piece = main[16 * k : 16 * k + 16]
                along_x = along_x + grade_x[k : k + 1] * piece
                along_y = along_y + weight_x[k : k + 1] * piece
                along_z = along_z + weight_x[k : k + 1] * tilt[16 * k : 16 * k + 16]
            forces[0].append(jnp.sum(along_x * weight_y, axis=0, keepdims=True))
            forces[1].append(jnp.sum(along_y * grade_y, axis=0, keepdims=True))
            forces[2].append(jnp.sum(along_z * weight_y, axis=0, keepdims=True))
        minus_q = -q_ref[rows, :]
        for d in range(3):
            out_ref[d, rows, :] = minus_q * jnp.concatenate(forces[d], axis=0)
        return carry

    lax.fori_loop(0, z_ref.shape[0] // 8, step, 0)


def modulus(index, length):
    coeffs = (1.0 / 120.0, 26.0 / 120.0, 66.0 / 120.0, 26.0 / 120.0, 1.0 / 120.0)
    real_part = 0.0
    imag_part = 0.0
    for j in range(5):
        angle = (index * j % length).astype(jnp.float32) * (2.0 * math.pi / length)
        real_part = real_part + coeffs[j] * jnp.cos(angle)
        imag_part = imag_part + coeffs[j] * jnp.sin(angle)
    return real_part * real_part + imag_part * imag_part


def influence(index_x, index_y, index_z):
    freq_x = jnp.where(2 * index_x < KX, index_x, index_x - KX).astype(jnp.float32) / KX
    freq_y = jnp.where(2 * index_y < KY, index_y, index_y - KY).astype(jnp.float32) / KY
    freq_z = jnp.where(2 * index_z < KZ, index_z, index_z - KZ).astype(jnp.float32) / KZ
    square = freq_x * freq_x + freq_y * freq_y + freq_z * freq_z
    safe = jnp.where(square > 0, square, 1.0)
    volume = float(KX * KY * KZ)
    value = jnp.exp(-math.pi**2 * safe / ewald_split**2) / (math.pi * volume * safe)
    value = value / (modulus(index_x, KX) * modulus(index_y, KY) * modulus(index_z, KZ))
    return jnp.where(square > 0, value, 0.0)


def waves(index, length):
    angle = (index % length) * (2.0 * math.pi / length)
    return (np.cos(angle), np.sin(angle))


def z_table(groups):
    planes = KZ // (2 * groups)
    frequency = np.arange(KZ // 2).reshape(groups, planes)
    cos, sin = waves(frequency[..., None] * np.arange(KZ), KZ)
    table = np.stack([cos, -sin], axis=1)
    table[0, 1, 0] = waves(np.arange(KZ) * (KZ // 2), KZ)[0]
    weight = np.full((groups, 2, planes), 2.0)
    weight[0, :, 0] = 1.0
    table = table.reshape(KZ, KZ)
    return (table.astype(np.float32), (table * weight.reshape(KZ, 1)).astype(np.float32))


def block_table(frequency, length, groups):
    position = np.arange(length)
    cos, sin = waves(frequency[..., None] * position, length)
    shape = (frequency.shape[0], frequency.shape[1], groups, length // groups)
    cos, sin = cos.reshape(shape), sin.reshape(shape)
    real_row = np.stack([cos, sin], axis=3)
    imag_row = np.stack([-sin, cos], axis=3)
    table = np.stack([real_row, imag_row], axis=1)
    return table.reshape(2 * length, 2 * length).astype(np.float32)


def y_frequency(groups):
    first = np.arange(KY // 2).reshape(groups, -1)
    second = np.where(first == 0, KY // 2, (KY - first) % KY)
    return np.concatenate([first, second], axis=1)


def exchange_kernel(axis, count, *refs):
    arrays = (len(refs) - 3) // 2
    sources, targets = refs[:arrays], refs[arrays : 2 * arrays]
    send_sem, recv_sem, own_sem = refs[2 * arrays :]
    me = lax.axis_index(axis)
    barrier = pltpu.get_barrier_semaphore()
    for d in range(1, count):
        pl.semaphore_signal(
            barrier,
            inc=1,
            device_id={axis: lax.rem(me + d, count)},
            device_id_type=pl.DeviceIdType.MESH,
        )
    pl.semaphore_wait(barrier, count - 1)
    copies = []
    for k in range(arrays):
        for d in range(1, count):
            peer = lax.rem(me + d, count)
            copies.append(
                pltpu.make_async_remote_copy(
                    src_ref=sources[k].at[peer],
                    dst_ref=targets[k].at[me],
                    send_sem=send_sem.at[k, d],
                    recv_sem=recv_sem.at[k, d],
                    device_id={axis: peer},
                    device_id_type=pl.DeviceIdType.MESH,
                )
            )
        copies.append(
            pltpu.make_async_copy(sources[k].at[me], targets[k].at[me], own_sem.at[k])
        )
    for copy in copies:
        copy.start()
    for copy in copies:
        copy.wait()


def exchange(arrays, axis, number):
    count = lax.axis_size(axis)
    vmem = pl.BlockSpec(memory_space=pltpu.VMEM)
    return pl.pallas_call(
        functools.partial(exchange_kernel, axis, count),
        out_shape=[jax.ShapeDtypeStruct(array.shape, array.dtype) for array in arrays],
        in_specs=[vmem] * len(arrays),
        out_specs=[vmem] * len(arrays),
        scratch_shapes=[
            pltpu.SemaphoreType.DMA((len(arrays), count)),
            pltpu.SemaphoreType.DMA((len(arrays), count)),
            pltpu.SemaphoreType.DMA((len(arrays),)),
        ],
        compiler_params=pltpu.CompilerParams(collective_id=number, has_side_effects=True),
        name="exchange" + str(number),
    )(*arrays)


def dot(left, right, left_dim, right_dim):
    dims = (((left_dim,), (right_dim,)), ((), ()))
    return lax.dot_general(
        left, right, dims, precision=highest, preferred_element_type=jnp.float32
    )


def spectrum_of(grid, block_x, block_y):
    grp, pen = lax.axis_size("grp"), lax.axis_size("pen")
    planes = KZ // (2 * pen)
    lines = KY // grp
    half = lines // 2
    forward_z, backward_z = z_table(pen)
    order_y = y_frequency(grp)
    table_y = block_table(order_y, KY, pen)
    table_x = block_table(np.arange(KX)[None], KX, grp)
    lines_z = dot(forward_z, grid.reshape(block_x * block_y, KZ), 1, 1)
    lines_z = lines_z.reshape(pen, 2, planes, block_x, block_y).transpose(0, 1, 4, 2, 3)
    (columns,) = exchange(
        [lines_z.reshape(pen, 2 * block_y, planes * block_x)], "pen", 1
    )
    lines_y = dot(table_y, columns.reshape(2 * KY, planes * block_x), 1, 0)
    lines_y = lines_y.reshape(grp, 2, lines, planes, block_x).transpose(0, 1, 4, 3, 2)
    (rows,) = exchange([lines_y.reshape(grp, 2 * block_x, planes * lines)], "grp", 2)
    rows = rows.reshape(grp, 2, block_x, planes * lines)
    at_grp, at_pen = lax.axis_index("grp"), lax.axis_index("pen")
    packed = rows[..., :lines]
    alone = (at_grp == 0) & (jnp.arange(lines) % half == 0)
    partner = jnp.where(
        alone, packed, jnp.concatenate([packed[..., half:], packed[..., :half]], axis=-1)
    )
    a, b = packed[:, :1], packed[:, 1:]
    c, d = partner[:, :1], partner[:, 1:]
    whole = jnp.concatenate([a + c, b - d], axis=1) * 0.5
    midway = jnp.concatenate([b + d, c - a], axis=1) * 0.5
    origin = at_pen == 0
    whole = jnp.where(origin, whole, packed)
    midway = jnp.where(origin, midway, 0.0)
    total_lanes = (planes + 1) * lines
    full = jnp.concatenate([whole, rows[..., lines:], midway], axis=-1)
    spectrum = dot(table_x, full.reshape(2 * KX, total_lanes), 1, 0)
    spectrum = spectrum.reshape(2, KX, total_lanes)
    index_x = jnp.arange(KX, dtype=jnp.int32)[:, None]
    slot = jnp.arange(planes + 1, dtype=jnp.int32)
    index_z = jnp.where(slot < planes, at_pen * planes + slot, KZ // 2)
    plane_weight = jnp.where(
        slot < planes,
        jnp.where(origin & (slot == 0), 1.0, 2.0),
        jnp.where(origin, 1.0, 0.0),
    )
    index_z = jnp.repeat(index_z, lines)[None, :]
    plane_weight = jnp.repeat(plane_weight, lines)[None, :]
    index_y = lax.dynamic_index_in_dim(jnp.asarray(order_y, jnp.int32), at_grp, 0, False)
    index_y = jnp.tile(index_y, planes + 1)[None, :]
    kernel = influence(index_x, index_y, index_z)
    power = spectrum[0] * spectrum[0] + spectrum[1] * spectrum[1]
    spectral = 0.5 * jnp.sum(plane_weight * kernel * power)
    scaled = (spectrum * kernel).reshape(2 * KX, total_lanes)
    returning = dot(table_x, scaled, 0, 0).reshape(grp, 2, block_x, total_lanes)
    midway = returning[..., planes * lines :]
    turned = jnp.concatenate([-midway[:, 1:], midway[:, :1]], axis=1)
    returning = jnp.concatenate(
        [returning[..., :lines] + turned, returning[..., lines : planes * lines]], axis=-1
    )
    rows, sums = exchange(
        [
            returning.reshape(grp, 2 * block_x, planes * lines),
            jnp.broadcast_to(spectral, (grp, 8, 128)),
        ],
        "grp",
        3,
    )
    spectral = jnp.sum(sums[:, 0, 0])
    rows = rows.reshape(grp, 2, block_x, planes, lines).transpose(0, 1, 4, 3, 2)
    columns = dot(table_y, rows.reshape(2 * KY, planes * block_x), 0, 0)
    columns, sums = exchange(
        [
            columns.reshape(pen, 2 * block_y, planes * block_x),
            jnp.broadcast_to(spectral, (pen, 8, 128)),
        ],
        "pen",
        4,
    )
    spectral = jnp.sum(sums[:, 0, 0])
    home = columns.reshape(pen, 2, block_y, planes, block_x).transpose(0, 1, 3, 4, 2)
    potential = dot(home.reshape(KZ, block_x * block_y), backward_z, 0, 0)
    return (potential.reshape(block_x, block_y, KZ), spectral)


def local(cell_offsets, cell_z, frac, charges, tile_counts):
    block_x = KX // lax.axis_size("grp")
    block_y = KY // lax.axis_size("pen")
    tiles = tile_counts.shape[0]
    slots = charges.shape[0] // tiles
    width = 4 * slots
    groups = tiles // 4
    per_row = block_y // 8
    live = jnp.arange(slots, dtype=jnp.int32)[None, :] < tile_counts[:, None]
    live_q = (charges.reshape(tiles, slots) * live.astype(jnp.float32)).reshape(groups, width)
    offsets = cell_offsets.reshape(2, groups, width)
    zcell = cell_z.reshape(groups, width)
    fracs = frac.reshape(3, groups, width)
    vmem = pl.BlockSpec(memory_space=pltpu.VMEM)
    params = pltpu.CompilerParams(vmem_limit_bytes=60 * 1024 * 1024)
    padded = pl.pallas_call(
        functools.partial(spread_kernel, per_row, slots),
        out_shape=jax.ShapeDtypeStruct((block_x + 8, block_y + 8, KZ), jnp.float32),
        in_specs=[vmem] * 4,
        out_specs=vmem,
        compiler_params=params,
        name="spread",
    )(offsets, zcell, fracs, live_q)
    rim_y = shifted(padded[: block_x + 5, block_y : block_y + 5], "pen", 1)
    merged = padded[: block_x + 5, :block_y].at[:, :5].add(rim_y)
    rim_x = shifted(merged[block_x : block_x + 5], "grp", 1)
    grid = merged[:block_x].at[:5].add(rim_x)
    potential, total = spectrum_of(grid, block_x, block_y)
    upper = shifted(potential[:5], "grp", -1)
    ext_x = jnp.concatenate([potential[:, :5], upper[:, :5]], axis=0)
    beside = shifted(ext_x, "pen", -1)
    beside = jnp.pad(beside, ((0, 0), (0, 3), (0, 0)))
    forces = pl.pallas_call(
        functools.partial(interp_kernel, per_row, slots),
        out_shape=jax.ShapeDtypeStruct((3, groups, width), jnp.float32),
        in_specs=[vmem] * 7,
        out_specs=vmem,
        scratch_shapes=[pltpu.VMEM((block_x + 8, block_y + 8, KZ), jnp.float32)],
        compiler_params=params,
        name="interp",
    )(offsets, zcell, fracs, live_q, potential, upper, beside)
    return (forces.reshape(3, groups * width), total / ATOMS)


def solution(mesh):
    in_specs = (
        P(None, ("grp", "pen")),
        P(("grp", "pen")),
        P(None, ("grp", "pen")),
        P(("grp", "pen")),
        P(("grp", "pen")),
    )
    out_specs = (P(None, ("grp", "pen")), P())
    return jax.shard_map(local, mesh=mesh, in_specs=in_specs, out_specs=out_specs, check_vma=False)
```
